32 devices in a mesh: bl: 4 (over y, x), freq: 8 (over z, core).
Axes of the slice: x: 2, y: 2, z: 4, core: 2. Of those that a mesh axis runs over, the one named last changes fastest.
Arguments:
- visibilities: float32 [2, 2, 128, 8192], P(None, None, 'freq', 'bl'), may hold values from -8 to 8
- sample_flag_weight: int32 [2, 128, 8192], P(None, 'freq', 'bl'), may hold values from 0 to 4
- baseline_station_pair: int32 [2, 8192], P(None, 'bl'), may hold values from 0 to 511, as said below
- baseline_spatial_coords: float32 [2, 2, 8192], P(None, None, 'bl'), may hold values from -6 to 6
- directions: float32 [2, 8], replicated, may hold values from -0.5 to 0.5
- source_flux: float32 [8, 128], P(None, 'freq'), may hold values from 0.5 to 2
- channel_ratio: float32 [128], P('freq'), may hold values from 0.7 to 1.4
- jones_gains: float32 [2, 8, 128, 512], P(None, None, 'freq'), may hold values from -4 to 4
- scaled_dual: float32 [2, 8, 128, 512], P(None, None, 'freq'), may hold values from -2 to 2
- consensus: float32 [2, 3, 8, 512], replicated, may hold values from -3 to 3
- penalty: float32 [8], replicated, may hold values from 0.3 to 3
Outputs:
- new_gains: float32 [2, 8, 128, 512], P(None, None, 'freq')
- new_consensus: float32 [2, 3, 8, 512], replicated
- new_dual: float32 [2, 8, 128, 512], P(None, None, 'freq')
- residuals: float32 [2, 2, 128, 8192], P(None, None, 'freq', 'bl')
The draws below stay inside these ranges and needn't reach their ends.
Inputs may be any that keep to these rules, and one draw needn't show every extreme that they name: `baseline_station_pair`: the two stations of every baseline differ.
All inputs are finite; a program needn't handle non-finite values.
Results may differ from the reference program's by a relative error of at most 0.00016.
Values sent between devices are 32-bit elements; how exact they have to be, the bound alone decides.
A program may use at most 64 MiB of HBM per device.

```python
import math
import jax
import jax.numpy as jnp
from jax import lax

STATION_TOTAL = 512
DIRS = 8
NPOLY = 3
ITERS = 3
TIME_SLOT_TOTAL = 2
BASELINE_TOTAL = 8192
CHANNEL_TOTAL = 128


def draw_baseline_station_pair(key, part):
    leading_dims = jax.random.randint(jax.random.fold_in(key, 11), (BASELINE_TOTAL,), 0, STATION_TOTAL)
    update_step_length = jax.random.randint(jax.random.fold_in(key, 12), (BASELINE_TOTAL,), 1, STATION_TOTAL)
    return jnp.stack([leading_dims, (leading_dims + update_step_length) % STATION_TOTAL]).astype(jnp.int32)


def set_ends(result, own_key, low, high):
    spot = [jax.random.randint(jax.random.fold_in(own_key, axis), (), 0, length) for axis, length in enumerate(result.shape)]
    widest = result.shape.index(max(result.shape))
    neighbour = spot[:widest] + [(spot[widest] + 1) % result.shape[widest]] + spot[widest + 1:]
    return result.at[tuple(spot)].set(low).at[tuple(neighbour)].set(high)


def level_of(key, dims, cuts, low, top_value):
    gain = 1.0
    for dim, shards_of in cuts:
        draws = jax.random.uniform(jax.random.fold_in(jax.random.fold_in(key, 6), dim), (shards_of,), jnp.float32, low / len(cuts), top_value / len(cuts))
        gain = gain * jnp.repeat(jnp.exp(draws), dims[dim] // shards_of).reshape((-1,) + (1,) * (len(dims) - 1 - dim))
    return gain


def gaussian(own_key, dims, spread, reach, cuts=(), held_as=jnp.bfloat16):
    values = jax.random.normal(own_key, dims, jnp.float32) * spread
    if len(cuts) > 0:
        values = level_of(own_key, dims, cuts, -0.22, 0.18) * values
    return jnp.clip(values, min=-reach, max=reach).astype(held_as)


def setup_inputs(seed: int = 0) -> dict:
    arg_keys = jax.random.split(jax.random.key(seed), 12)
    return {
        "visibilities": gaussian(arg_keys[0], (2, TIME_SLOT_TOTAL, CHANNEL_TOTAL, BASELINE_TOTAL), 1.0, 8.0, ((2, 8), (3, 4)), jnp.float32),
        "sample_flag_weight": set_ends(jax.random.randint(arg_keys[1], (TIME_SLOT_TOTAL, CHANNEL_TOTAL, BASELINE_TOTAL), 0, 5), jax.random.fold_in(arg_keys[1], 1), 0, 4).astype(jnp.int32),
        "baseline_station_pair": draw_baseline_station_pair(jax.random.fold_in(arg_keys[11], 71), 0),
        "baseline_spatial_coords": gaussian(arg_keys[3], (2, TIME_SLOT_TOTAL, BASELINE_TOTAL), 1.0, 6.0, ((2, 4),), jnp.float32),
        "directions": jnp.clip(jax.random.uniform(arg_keys[4], (2, DIRS), jnp.float32, -0.5, 0.5), -0.5, 0.5),
        "source_flux": jnp.clip(jnp.exp(math.log(2.0) - 1.3862944 * jax.random.uniform(arg_keys[5], (DIRS, CHANNEL_TOTAL), jnp.float32) ** level_of(arg_keys[5], (DIRS, CHANNEL_TOTAL), ((1, 8),), -0.2, 0.2)), 0.5, 2.0),
        "channel_ratio": jnp.clip(jnp.exp(math.log(1.4) - 0.6931472 * jax.random.uniform(arg_keys[6], (CHANNEL_TOTAL,), jnp.float32) ** level_of(arg_keys[6], (CHANNEL_TOTAL,), ((0, 8),), -0.2, 0.2)), 0.7, 1.4),
        "jones_gains": gaussian(arg_keys[7], (2, DIRS, CHANNEL_TOTAL, STATION_TOTAL), 0.8, 4.0, ((2, 8),), jnp.float32),
        "scaled_dual": gaussian(arg_keys[8], (2, DIRS, CHANNEL_TOTAL, STATION_TOTAL), 0.3, 2.0, ((2, 8),), jnp.float32),
        "consensus": gaussian(arg_keys[9], (2, NPOLY, DIRS, STATION_TOTAL), 0.5, 3.0, (), jnp.float32),
        "penalty": jnp.clip(jnp.exp(jax.random.uniform(arg_keys[10], (DIRS,), jnp.float32, math.log(0.3), math.log(3.0))), 0.3, 3.0),
    }


robust_dof = 2.0
small_term = 1e-06
two_pi = 2.0 * math.pi

def legendre(ratios):
    scaled = (ratios - 1.05) / 0.35
    values = [jnp.ones_like(scaled), scaled]
    for degree in range(1, NPOLY - 1):
        values.append(((2 * degree + 1) * scaled * values[degree] - degree * values[degree - 1]) / (degree + 1))
    return jnp.stack(values[:NPOLY])

def coherency(coords, sky_dirs, fluxes, ratios):
    project = sky_dirs[0][:, None, None] * coords[0][None] + sky_dirs[1][:, None, None] * coords[1][None]
    phases = two_pi * project[:, :, None, :] * ratios[None, None, :, None]
    amplitude = fluxes[:, None, :, None]
    return (amplitude * jnp.cos(phases), amplitude * jnp.sin(phases))

def predict(gain_re, gain_im, pair_index, sky_re, sky_im):
    left_re = jnp.take(gain_re, pair_index[0], axis=2)
    left_im = jnp.take(gain_im, pair_index[0], axis=2)
    right_re = jnp.take(gain_re, pair_index[1], axis=2)
    right_im = jnp.take(gain_im, pair_index[1], axis=2)
    pair_re = left_re * right_re + left_im * right_im
    pair_im = left_im * right_re - left_re * right_im
    model_re = pair_re[:, None] * sky_re - pair_im[:, None] * sky_im
    model_im = pair_re[:, None] * sky_im + pair_im[:, None] * sky_re
    return ((left_re, left_im, right_re, right_im), model_re, model_im)

def residual_of(observed, model_re, model_im):
    return (observed[0] - jnp.sum(model_re, axis=0), observed[1] - jnp.sum(model_im, axis=0))

def robust_weights(flagged, error_re, error_im, sigma_sq):
    return flagged * (robust_dof + 1.0) / (robust_dof + (error_re * error_re + error_im * error_im) / sigma_sq)

def normal_terms(error_re, error_im, model_re, model_im, weights, sky_re, sky_im, side_gains, pair_index, station_list):
    target_re = error_re[None] + model_re
    target_im = error_im[None] + model_im
    cross_re = sky_re * target_re + sky_im * target_im
    cross_im = sky_re * target_im - sky_im * target_re
    weight_wide = weights[None]
    summed_re = jnp.sum(weight_wide * cross_re, axis=1)
    summed_im = jnp.sum(weight_wide * cross_im, axis=1)
    powers = jnp.sum(weight_wide * (sky_re * sky_re + sky_im * sky_im), axis=1)
    left_re, left_im, right_re, right_im = side_gains
    first_re = right_re * summed_re - right_im * summed_im
    first_im = right_re * summed_im + right_im * summed_re
    second_re = left_re * summed_re + left_im * summed_im
    second_im = left_im * summed_re - left_re * summed_im
    first_norm = (right_re * right_re + right_im * right_im) * powers
    second_norm = (left_re * left_re + left_im * left_im) * powers
    stacked_first = jnp.stack([first_re, first_im, first_norm])
    stacked_second = jnp.stack([second_re, second_im, second_norm])
    zeroed = jnp.zeros(stacked_first.shape[:3] + (station_list,), stacked_first.dtype)
    return zeroed.at[:, :, :, pair_index[0]].add(stacked_first).at[:, :, :, pair_index[1]].add(stacked_second)

def update_gains(gain_re, gain_im, normal_sums, anchor_re, anchor_im, effective_penalty):
    penalty_wide = effective_penalty[:, None, None]
    divisor = normal_sums[2] + penalty_wide
    solved_re = (normal_sums[0] + penalty_wide * anchor_re) / divisor
    solved_im = (normal_sums[1] + penalty_wide * anchor_im) / divisor
    return (0.5 * (gain_re + solved_re), 0.5 * (gain_im + solved_im))

def cholesky_solve(gram_total, flat_rhs):
    factor = jnp.linalg.cholesky(gram_total)
    matrix_order = gram_total.shape[0]
    forward = []
    for row_index in range(matrix_order):
        running = flat_rhs[row_index]
        for col_index in range(row_index):
            running = running - factor[row_index, col_index] * forward[col_index]
        forward.append(running / factor[row_index, row_index])
    backward = [None] * matrix_order
    for row_index in reversed(range(matrix_order)):
        running = forward[row_index]
        for col_index in range(row_index + 1, matrix_order):
            running = running - factor[col_index, row_index] * backward[col_index]
        backward[row_index] = running / factor[row_index, row_index]
    return jnp.stack(backward)

def solve_consensus(gram_total, rhs_total):
    matrix_order = gram_total.shape[0]
    flat_rhs = jnp.moveaxis(rhs_total, 1, 0).reshape(matrix_order, -1)
    solved = cholesky_solve(gram_total, flat_rhs)
    return jnp.moveaxis(solved.reshape((matrix_order, rhs_total.shape[0]) + rhs_total.shape[2:]), 0, 1)

def reference(visibilities, sample_flag_weight, baseline_station_pair, baseline_spatial_coords, directions, source_flux, channel_ratio, jones_gains, scaled_dual, consensus, penalty):
    chan_block = math.gcd(CHANNEL_TOTAL, 8)
    blocks = CHANNEL_TOTAL // chan_block

    def split_axis(tensor, position):
        old_shape = tensor.shape
        reshaped = tensor.reshape(old_shape[:position] + (blocks, chan_block) + old_shape[position + 1:])
        return jnp.moveaxis(reshaped, position, 0)

    def join_axis(tensor, position):
        moved_axes = jnp.moveaxis(tensor, 0, position)
        old_shape = moved_axes.shape
        return moved_axes.reshape(old_shape[:position] + (blocks * chan_block,) + old_shape[position + 2:])
    effective_penalty = penalty * (2.0 * BASELINE_TOTAL * TIME_SLOT_TOTAL / STATION_TOTAL)
    poly_basis = legendre(channel_ratio)
    anchor = jnp.einsum('jc,xjks->xkcs', poly_basis, consensus, precision=lax.Precision.HIGHEST) - scaled_dual
    flagged = sample_flag_weight.astype(jnp.float32)
    weight_count = jnp.sum(flagged)
    vis_blocks = split_axis(visibilities, 2)
    flag_blocks = split_axis(flagged, 1)
    flux_blocks = split_axis(source_flux, 1)
    ratio_blocks = channel_ratio.reshape(blocks, chan_block)
    anchor_blocks = split_axis(anchor, 2)

    def block_model(gain_block, flux_block, ratio_block):
        sky_re, sky_im = coherency(baseline_spatial_coords, directions, flux_block, ratio_block)
        side_gains, model_re, model_im = predict(gain_block[0], gain_block[1], baseline_station_pair, sky_re, sky_im)
        return (sky_re, sky_im, side_gains, model_re, model_im)
    gain_state = jones_gains
    for iteration in range(ITERS):
        gain_blocks = split_axis(gain_state, 2)

        def misfit_block(block_items):
            vis_block, flag_block, flux_block, ratio_block, gain_block = block_items
            sky_re, sky_im, side_gains, model_re, model_im = block_model(gain_block, flux_block, ratio_block)
            error_re, error_im = residual_of(vis_block, model_re, model_im)
            return jnp.sum(flag_block * (error_re * error_re + error_im * error_im))
        squares = jnp.sum(lax.map(misfit_block, (vis_blocks, flag_blocks, flux_blocks, ratio_blocks, gain_blocks)))
        sigma_sq = squares / (weight_count + 1.0) + small_term

        def update_block(block_items):
            vis_block, flag_block, flux_block, ratio_block, gain_block, anchor_block = block_items
            sky_re, sky_im, side_gains, model_re, model_im = block_model(gain_block, flux_block, ratio_block)
            error_re, error_im = residual_of(vis_block, model_re, model_im)
            weights = robust_weights(flag_block, error_re, error_im, sigma_sq)
            normal_sums = normal_terms(error_re, error_im, model_re, model_im, weights, sky_re, sky_im, side_gains, baseline_station_pair, STATION_TOTAL)
            new_re, new_im = update_gains(gain_block[0], gain_block[1], normal_sums, anchor_block[0], anchor_block[1], effective_penalty)
            return jnp.stack([new_re, new_im])
        gain_state = join_axis(lax.map(update_block, (vis_blocks, flag_blocks, flux_blocks, ratio_blocks, gain_blocks, anchor_blocks)), 2)
    final_blocks = split_axis(gain_state, 2)

    def residual_block(block_items):
        vis_block, flux_block, ratio_block, gain_block = block_items
        sky_re, sky_im, side_gains, model_re, model_im = block_model(gain_block, flux_block, ratio_block)
        error_re, error_im = residual_of(vis_block, model_re, model_im)
        return jnp.stack([error_re, error_im])
    residuals = join_axis(lax.map(residual_block, (vis_blocks, flux_blocks, ratio_blocks, final_blocks)), 2)
    gram_total = jnp.dot(poly_basis, poly_basis.T, precision=lax.Precision.HIGHEST)
    rhs_total = jnp.einsum('jc,xkcs->xjks', poly_basis, gain_state + scaled_dual, precision=lax.Precision.HIGHEST)
    new_consensus = solve_consensus(gram_total, rhs_total)
    new_dual = scaled_dual + gain_state - jnp.einsum('jc,xjks->xkcs', poly_basis, new_consensus, precision=lax.Precision.HIGHEST)
    return (gain_state, new_consensus, new_dual, residuals)
```

```python
import functools
import math

import jax
import jax.numpy as jnp
from jax import lax
from jax.experimental import pallas as pl
from jax.experimental.pallas import tpu as pltpu
from jax.sharding import PartitionSpec as P

NPOLY = 3
ITERS = 3

robust_dof = 2.0
small_term = 1e-06
two_pi = 2.0 * math.pi
MESH = pl.DeviceIdType.MESH

SIN_TERMS = [(-1.0) ** n * two_pi ** (2 * n + 1) / math.factorial(2 * n + 1) for n in range(6)]
COS_TERMS = [(-1.0) ** n * two_pi ** (2 * n) / math.factorial(2 * n) for n in range(7)]


def horner(terms, square):
    value = jnp.full_like(square, terms[-1])
    for term in terms[-2::-1]:
        value = value * square + term
    return value


def turn_parts(turns):
    half = jnp.floor(turns * 2.0 + 0.5)
    rest = turns - half * 0.5
    sign = 1.0 - 2.0 * (half - 2.0 * jnp.floor(half * 0.5))
    square = rest * rest
    return horner(COS_TERMS, square), rest * horner(SIN_TERMS, square), sign


def column(row, count):
    spread = jnp.broadcast_to(row, (count, count))
    r = lax.broadcasted_iota(jnp.int32, (count, count), 0)
    c = lax.broadcasted_iota(jnp.int32, (count, count), 1)
    return jnp.sum(jnp.where(r == c, spread, 0.0), axis=1, keepdims=True)


def split_two(value):
    high = value.astype(jnp.bfloat16)
    low = (value - high.astype(jnp.float32)).astype(jnp.bfloat16)
    return high, low


def kernel(
    sizes,
    vis,
    flag,
    pair,
    coords,
    dirs,
    flux,
    ratio,
    gains_in,
    dual,
    cons_in,
    penalty,
    gains_out,
    cons_out,
    dual_out,
    resid_out,
    table,
    sky,
    side,
    gsplit,
    err,
    weighted,
    wsum,
    flux_sq,
    stacked,
    partial,
    rs_buf,
    gains,
    s_bl,
    s_fr,
    c_fr,
    c_bl,
    rs_send,
    rs_recv,
    ag_send,
    ag_recv,
    sb_send,
    sb_recv,
    sf_send,
    sf_recv,
    cf_send,
    cf_recv,
    cb_send,
    cb_recv,
):
    nb, nf, slots, chans, base, dirn, stations, ch, rho_scale = sizes
    kb = dirn // nb
    chunks = base // ch
    me = lax.axis_index("bl")
    mf = lax.axis_index("freq")
    own = me * kb

    barrier = pltpu.get_barrier_semaphore()
    for o in range(1, nb):
        pl.semaphore_signal(
            barrier, inc=1, device_id={"bl": lax.rem(me + o, nb)}, device_id_type=MESH
        )
    for o in range(1, nf):
        pl.semaphore_signal(
            barrier, inc=1, device_id={"freq": lax.rem(mf + o, nf)}, device_id_type=MESH
        )

    def remote(src, dst, send, recv, axis, target):
        return pltpu.make_async_remote_copy(
            src_ref=src,
            dst_ref=dst,
            send_sem=send,
            recv_sem=recv,
            device_id={axis: target},
            device_id_type=MESH,
        )

    ratio_col = column(ratio[...], chans)
    scaled = (ratio_col - 1.05) / 0.35
    basis = [jnp.ones_like(scaled), scaled, (3.0 * scaled * scaled - 1.0) / 2.0]
    flux_cols = [column(flux[k : k + 1, :], chans) for k in range(dirn)]
    for k in range(dirn):
        flux_sq[k] = jnp.broadcast_to(flux_cols[k] * flux_cols[k], (chans, ch))

    def setup(i, count):
        at = pl.multiple_of(i * ch, ch)
        cols = pl.ds(at, ch)
        rows = lax.broadcasted_iota(jnp.int32, (stations, ch), 0)
        for s in range(2):
            hit = rows == pair[s : s + 1, cols]
            table[:, pl.ds(pl.multiple_of(s * base + at, ch), ch)] = jnp.where(
                hit, 1.0, 0.0
            ).astype(jnp.bfloat16)
        for t in range(slots):
            u = coords[0, t : t + 1, cols]
            v = coords[1, t : t + 1, cols]
            for k in range(dirn):
                project = dirs[0, k] * u + dirs[1, k] * v
                cosine, sine, sign = turn_parts(project * ratio_col)
                amplitude = sign * flux_cols[k]
                sky[0, k, t, :, cols] = amplitude * cosine
                sky[1, k, t, :, cols] = amplitude * sine
            count = count + tile_sum(flag[t, :, cols].astype(jnp.float32))
        return count

    def tile_sum(value):
        total = value[:8]
        for r in range(8, chans, 8):
            total = total + value[r : r + 8]
        out = total[:, :128]
        for c in range(128, ch, 128):
            out = out + total[:, c : c + 128]
        return out

    count = lax.fori_loop(0, chunks, setup, jnp.zeros((8, 128), jnp.float32))
    for it in range(ITERS):
        s_bl[it, me, 1] = count
    gains[0] = gains_in[...]

    pl.semaphore_wait(barrier, nb + nf - 2)

    def predict(it, target):
        high, low = split_two(gains[it].reshape(2 * dirn * chans, stations))
        gsplit[0] = high
        gsplit[1] = low

        def step(i, misfit):
            at = pl.multiple_of(i * ch, ch)
            cols = pl.ds(at, ch)
            left = gsplit[...].reshape(2 * 2 * dirn * chans, stations)
            half = 2 * dirn * chans
            for s in range(2):
                where = pl.ds(pl.multiple_of(s * base + at, ch), ch)
                both = jnp.dot(left, table[:, where], preferred_element_type=jnp.float32)
                side[:, :, :, where] = (both[:half] + both[half:]).reshape(2, dirn, chans, ch)
            right = pl.ds(pl.multiple_of(base + at, ch), ch)
            er = [vis[0, t, :, cols] for t in range(slots)]
            ei = [vis[1, t, :, cols] for t in range(slots)]
            for k in range(dirn):
                lr, li = side[0, k, :, cols], side[1, k, :, cols]
                rr, ri = side[0, k, :, right], side[1, k, :, right]
                pr = lr * rr + li * ri
                pi = li * rr - lr * ri
                for t in range(slots):
                    sr, si = sky[0, k, t, :, cols], sky[1, k, t, :, cols]
                    er[t] = er[t] - (pr * sr - pi * si)
                    ei[t] = ei[t] - (pr * si + pi * sr)
            for t in range(slots):
                target[0, t, :, cols] = er[t]
                target[1, t, :, cols] = ei[t]
                power = er[t] * er[t] + ei[t] * ei[t]
                misfit = misfit + tile_sum(flag[t, :, cols].astype(jnp.float32) * power)
            return misfit

        return lax.fori_loop(0, chunks, step, jnp.zeros((8, 128), jnp.float32))

    def iteration(it, carry):
        s_bl[it, me, 0] = predict(it, err)
        copies = [
            remote(
                s_bl.at[it, me], s_bl.at[it, me], sb_send.at[it, o], sb_recv.at[it, o],
                "bl", lax.rem(me + o, nb),
            )
            for o in range(1, nb)
        ]
        for copy in copies:
            copy.start()
        for copy in copies:
            copy.wait_recv()
        total = s_bl[it, 0]
        for o in range(1, nb):
            total = total + s_bl[it, o]
        s_fr[it, mf] = total
        more = [
            remote(
                s_fr.at[it, mf], s_fr.at[it, mf], sf_send.at[it, o], sf_recv.at[it, o],
                "freq", lax.rem(mf + o, nf),
            )
            for o in range(1, nf)
        ]
        for copy in more:
            copy.start()
        for copy in more:
            copy.wait_recv()
        total = s_fr[it, 0]
        for o in range(1, nf):
            total = total + s_fr[it, o]
        lanes = jnp.sum(total, axis=2, keepdims=True)
        sums = jnp.sum(lanes, axis=1, keepdims=True)
        sigma_sq = sums[0] / (sums[1] + 1.0) + small_term
        inverse = 1.0 / sigma_sq

        def weigh(i, carry):
            cols = pl.ds(pl.multiple_of(i * ch, ch), ch)
            total = None
            for t in range(slots):
                er, ei = err[0, t, :, cols], err[1, t, :, cols]
                power = er * er + ei * ei
                r = (
                    flag[t, :, cols].astype(jnp.float32)
                    * (robust_dof + 1.0)
                    / (robust_dof + power * inverse)
                )
                weighted[0, t, :, cols] = r * er
                weighted[1, t, :, cols] = r * ei
                total = r if total is None else total + r
            wsum[:, cols] = total
            return carry

        lax.fori_loop(0, chunks, weigh, 0)

        sends = []
        for o in list(range(1, nb)) + [0]:
            owner = lax.rem(me + o, nb)
            first = owner * kb

            def normal(i, carry, first=first):
                at = pl.multiple_of(i * ch, ch)
                cols = pl.ds(at, ch)
                right = pl.ds(pl.multiple_of(base + at, ch), ch)
                for kk in range(kb):
                    k = first + kk
                    lr, li = side[0, k, :, cols], side[1, k, :, cols]
                    rr, ri = side[0, k, :, right], side[1, k, :, right]
                    c2 = flux_sq[k] * wsum[:, cols]
                    xr = (lr * rr + li * ri) * c2
                    xi = (li * rr - lr * ri) * c2
                    for t in range(slots):
                        sr, si = sky[0, k, t, :, cols], sky[1, k, t, :, cols]
                        wr, wi = weighted[0, t, :, cols], weighted[1, t, :, cols]
                        xr = xr + (sr * wr + si * wi)
                        xi = xi + (sr * wi - si * wr)
                    terms = (
                        (rr * xr - ri * xi, lr * xr + li * xi),
                        (rr * xi + ri * xr, li * xr - lr * xi),
                        ((rr * rr + ri * ri) * c2, (lr * lr + li * li) * c2),
                    )
                    for q in range(3):
                        for s, where in enumerate((cols, right)):
                            high, low = split_two(terms[q][s])
                            stacked[0, q, kk, :, where] = high
                            stacked[1, q, kk, :, where] = low
                return carry

            lax.fori_loop(0, chunks, normal, 0)
            half = 3 * kb * chans
            both = lax.dot_general(
                stacked[...].reshape(2 * half, 2 * base),
                table[...],
                (((1,), (1,)), ((), ())),
                preferred_element_type=jnp.float32,
            )
            partial[it, o] = (both[:half] + both[half:]).reshape(3, kb, chans, stations)
            if o > 0:
                copy = remote(
                    partial.at[it, o], rs_buf.at[it, o], rs_send.at[it, o], rs_recv.at[it, o],
                    "bl", owner,
                )
                copy.start()
                sends.append(copy)
        for copy in sends:
            copy.wait_recv()

        for kk in range(kb):
            k = own + kk
            rho = penalty[k] * rho_scale
            sums_k = []
            for q in range(3):
                value = partial[it, 0, q, kk]
                for o in range(1, nb):
                    value = value + rs_buf[it, o, q, kk]
                sums_k.append(value)
            divisor = 1.0 / (sums_k[2] + rho)
            for c in range(2):
                anchor = -dual[c, k]
                for j in range(NPOLY):
                    anchor = anchor + basis[j] * cons_in[c, j, pl.ds(k, 1), :]
                solved = (sums_k[c] + rho * anchor) * divisor
                gains[it + 1, c, k] = 0.5 * (gains[it, c, k] + solved)
        block = gains.at[it + 1, :, pl.ds(own, kb)]
        spread = [
            remote(
                block, block, ag_send.at[it, o], ag_recv.at[it, o], "bl", lax.rem(me + o, nb)
            )
            for o in range(1, nb)
        ]
        for copy in spread:
            copy.start()
        for copy in spread:
            copy.wait_recv()
        for copy in copies + more + sends + spread:
            copy.wait_send()
        return carry

    lax.fori_loop(0, ITERS, iteration, 0)

    rows = 2 * NPOLY * kb
    for c in range(2):
        for kk in range(kb):
            both = gains[ITERS, c, own + kk] + dual[c, own + kk]
            for j in range(NPOLY):
                row = (c * NPOLY + j) * kb + kk
                c_fr[mf, row : row + 1, :] = jnp.sum(basis[j] * both, axis=0, keepdims=True)
    grams = [(a, b) for a in range(NPOLY) for b in range(a + 1)]
    for n, (a, b) in enumerate(grams):
        entry = jnp.sum(basis[a] * basis[b], axis=0, keepdims=True)
        c_fr[mf, rows + n : rows + n + 1, :] = jnp.broadcast_to(entry, (1, stations))
    for row in range(rows + len(grams), c_fr.shape[1]):
        c_fr[mf, row : row + 1, :] = jnp.zeros((1, stations), jnp.float32)
    more = [
        remote(
            c_fr.at[mf], c_fr.at[mf], cf_send.at[o], cf_recv.at[o], "freq", lax.rem(mf + o, nf)
        )
        for o in range(1, nf)
    ]
    for copy in more:
        copy.start()

    predict(ITERS, resid_out)
    gains_out[...] = gains[ITERS]

    for copy in more:
        copy.wait_recv()
    total = c_fr[0]
    for o in range(1, nf):
        total = total + c_fr[o]
    gram = {ab: total[rows + n : rows + n + 1] for n, ab in enumerate(grams)}
    factor = {}
    for a in range(NPOLY):
        for b in range(a + 1):
            value = gram[a, b]
            for m in range(b):
                value = value - factor[a, m] * factor[b, m]
            factor[a, b] = jnp.sqrt(value) if a == b else value / factor[b, b]
    for c in range(2):
        part = [
            total[(c * NPOLY + j) * kb : (c * NPOLY + j + 1) * kb] for j in range(NPOLY)
        ]
        forward = []
        for a in range(NPOLY):
            running = part[a]
            for b in range(a):
                running = running - factor[a, b] * forward[b]
            forward.append(running / factor[a, a])
        backward = [None] * NPOLY
        for a in reversed(range(NPOLY)):
            running = forward[a]
            for b in range(a + 1, NPOLY):
                running = running - factor[b, a] * backward[b]
            backward[a] = running / factor[a, a]
        for j in range(NPOLY):
            row = (c * NPOLY + j) * kb
            c_bl[me, row : row + kb, :] = backward[j]
    for row in range(rows, c_bl.shape[1]):
        c_bl[me, row : row + 1, :] = jnp.zeros((1, stations), jnp.float32)
    spread = [
        remote(
            c_bl.at[me], c_bl.at[me], cb_send.at[o], cb_recv.at[o], "bl", lax.rem(me + o, nb)
        )
        for o in range(1, nb)
    ]
    for copy in spread:
        copy.start()
    for copy in spread:
        copy.wait_recv()
    for g in range(nb):
        for kk in range(kb):
            k = g * kb + kk
            for c in range(2):
                value = dual[c, k] + gains[ITERS, c, k]
                for j in range(NPOLY):
                    row = (c * NPOLY + j) * kb + kk
                    coefficient = c_bl[g, row : row + 1, :]
                    cons_out[c, j, k : k + 1, :] = coefficient
                    value = value - basis[j] * coefficient
                dual_out[c, k] = value
    for copy in more + spread:
        copy.wait_send()


def body(nb, nf, vis, flag, pair, coords, dirs, flux, ratio, gains, dual, cons, penalty):
    f32, bf16 = jnp.float32, jnp.bfloat16
    _, slots, chans, base = vis.shape
    dirn, stations = gains.shape[1], gains.shape[3]
    kb = dirn // nb
    ch = 256
    rho_scale = 2.0 * base * nb * slots / stations
    sizes = (nb, nf, slots, chans, base, dirn, stations, ch, rho_scale)
    pad = lambda n: -(-n // 8) * 8
    rows = 2 * NPOLY * kb
    vmem = pl.BlockSpec(memory_space=pltpu.VMEM)
    smem = pl.BlockSpec(memory_space=pltpu.SMEM)
    dma = pltpu.SemaphoreType.DMA
    shape = jax.ShapeDtypeStruct
    return pl.pallas_call(
        functools.partial(kernel, sizes),
        name="admm_step",
        out_shape=(
            shape(gains.shape, f32),
            shape(cons.shape, f32),
            shape(dual.shape, f32),
            shape(vis.shape, f32),
        ),
        in_specs=[vmem, vmem, vmem, vmem, smem, vmem, vmem, vmem, vmem, vmem, smem],
        out_specs=(vmem, vmem, vmem, vmem),
        scratch_shapes=[
            pltpu.VMEM((stations, 2 * base), bf16),
            pltpu.VMEM((2, dirn, slots, chans, base), f32),
            pltpu.VMEM((2, dirn, chans, 2 * base), f32),
            pltpu.VMEM((2, 2 * dirn * chans, stations), bf16),
            pltpu.VMEM((2, slots, chans, base), f32),
            pltpu.VMEM((2, slots, chans, base), f32),
            pltpu.VMEM((chans, base), f32),
            pltpu.VMEM((dirn, chans, ch), f32),
            pltpu.VMEM((2, 3, kb, chans, 2 * base), bf16),
            pltpu.VMEM((ITERS, nb, 3, kb, chans, stations), f32),
            pltpu.VMEM((ITERS, nb, 3, kb, chans, stations), f32),
            pltpu.VMEM((ITERS + 1,) + gains.shape, f32),
            pltpu.VMEM((ITERS, nb, 2, 8, 128), f32),
            pltpu.VMEM((ITERS, nf, 2, 8, 128), f32),
            pltpu.VMEM((nf, pad(rows + 6), stations), f32),
            pltpu.VMEM((nb, pad(rows), stations), f32),
            dma((ITERS, nb)),
            dma((ITERS, nb)),
            dma((ITERS, nb)),
            dma((ITERS, nb)),
            dma((ITERS, nb)),
            dma((ITERS, nb)),
            dma((ITERS, nf)),
            dma((ITERS, nf)),
            dma((nf,)),
            dma((nf,)),
            dma((nb,)),
            dma((nb,)),
        ],
        compiler_params=pltpu.CompilerParams(
            collective_id=0, has_side_effects=True, vmem_limit_bytes=60 * 1024 * 1024
        ),
    )(vis, flag, pair, coords, dirs, flux, ratio.reshape(1, -1), gains, dual, cons, penalty)


def solution(mesh):
    in_specs = (
        P(None, None, "freq", "bl"),
        P(None, "freq", "bl"),
        P(None, "bl"),
        P(None, None, "bl"),
        P(),
        P(None, "freq"),
        P("freq"),
        P(None, None, "freq", None),
        P(None, None, "freq", None),
        P(),
        P(),
    )
    out_specs = (
        P(None, None, "freq", None),
        P(),
        P(None, None, "freq", None),
        P(None, None, "freq", "bl"),
    )
    step = functools.partial(body, mesh.shape["bl"], mesh.shape["freq"])
    return jax.shard_map(step, mesh=mesh, in_specs=in_specs, out_specs=out_specs, check_vma=False)
```

```python
import functools
import math

import jax
import jax.numpy as jnp
from jax import lax
from jax.experimental import pallas as pl
from jax.experimental.pallas import tpu as pltpu
from jax.sharding import PartitionSpec as P

NPOLY = 3
ITERS = 3

robust_dof = 2.0
small_term = 1e-06
two_pi = 2.0 * math.pi
MESH = pl.DeviceIdType.MESH

SIN_TERMS = [(-1.0) ** n * two_pi ** (2 * n + 1) / math.factorial(2 * n + 1) for n in range(6)]
COS_TERMS = [(-1.0) ** n * two_pi ** (2 * n) / math.factorial(2 * n) for n in range(7)]


def horner(terms, square):
    value = jnp.full_like(square, terms[-1])
    for term in terms[-2::-1]:
        value = value * square + term
    return value


def turn_parts(turns):
    half = jnp.floor(turns * 2.0 + 0.5)
    rest = turns - half * 0.5
    sign = 1.0 - 2.0 * (half - 2.0 * jnp.floor(half * 0.5))
    square = rest * rest
    return horner(COS_TERMS, square), rest * horner(SIN_TERMS, square), sign


def column(row, count):
    spread = jnp.broadcast_to(row, (count, count))
    r = lax.broadcasted_iota(jnp.int32, (count, count), 0)
    c = lax.broadcasted_iota(jnp.int32, (count, count), 1)
    return jnp.sum(jnp.where(r == c, spread, 0.0), axis=1, keepdims=True)


def split_two(value):
    high = value.astype(jnp.bfloat16)
    low = (value - high.astype(jnp.float32)).astype(jnp.bfloat16)
    return high, low


def kernel(
    sizes,
    vis,
    flag,
    pair,
    coords,
    dirs,
    flux,
    ratio,
    gains_in,
    dual,
    cons_in,
    penalty,
    gains_out,
    cons_out,
    dual_out,
    resid_out,
    table,
    sky,
    side,
    gsplit,
    err,
    weighted,
    wsum,
    flux_sq,
    stacked,
    partial,
    rs_buf,
    gains,
    s_bl,
    s_fr,
    c_fr,
    c_bl,
    rs_send,
    rs_recv,
    ag_send,
    ag_recv,
    sb_send,
    sb_recv,
    sf_send,
    sf_recv,
    cf_send,
    cf_recv,
    cb_send,
    cb_recv,
):
    nb, nf, slots, chans, base, dirn, stations, ch, rho_scale = sizes
    kb = dirn // nb
    chunks = base // ch
    me = lax.axis_index("bl")
    mf = lax.axis_index("freq")
    own = me * kb

    def bl_peer(o):
        return lax.bitwise_xor(me, o)

    barrier = pltpu.get_barrier_semaphore()
    for o in range(1, nb):
        pl.semaphore_signal(
            barrier, inc=1, device_id={"bl": bl_peer(o)}, device_id_type=MESH
        )
    for o in range(1, nf):
        pl.semaphore_signal(
            barrier, inc=1, device_id={"freq": lax.rem(mf + o, nf)}, device_id_type=MESH
        )

    def remote(src, dst, send, recv, axis, target):
        return pltpu.make_async_remote_copy(
            src_ref=src,
            dst_ref=dst,
            send_sem=send,
            recv_sem=recv,
            device_id={axis: target},
            device_id_type=MESH,
        )

    ratio_col = column(ratio[...], chans)
    scaled = (ratio_col - 1.05) / 0.35
    basis = [jnp.ones_like(scaled), scaled, (3.0 * scaled * scaled - 1.0) / 2.0]
    flux_cols = [column(flux[k : k + 1, :], chans) for k in range(dirn)]
    for k in range(dirn):
        flux_sq[k] = jnp.broadcast_to(flux_cols[k] * flux_cols[k], (chans, ch))

    def setup(i, count):
        at = pl.multiple_of(i * ch, ch)
        cols = pl.ds(at, ch)
        rows = lax.broadcasted_iota(jnp.int32, (stations, ch), 0)
        for s in range(2):
            hit = rows == pair[s : s + 1, cols]
            table[:, pl.ds(pl.multiple_of(s * base + at, ch), ch)] = jnp.where(
                hit, 1.0, 0.0
            ).astype(jnp.bfloat16)
        for t in range(slots):
            u = coords[0, t : t + 1, cols]
            v = coords[1, t : t + 1, cols]
            for k in range(dirn):
                project = dirs[0, k] * u + dirs[1, k] * v
                cosine, sine, sign = turn_parts(project * ratio_col)
                amplitude = sign * flux_cols[k]
                sky[0, k, t, :, cols] = amplitude * cosine
                sky[1, k, t, :, cols] = amplitude * sine
            count = count + tile_sum(flag[t, :, cols].astype(jnp.float32))
        return count

    def tile_sum(value):
        total = value[:8]
        for r in range(8, chans, 8):
            total = total + value[r : r + 8]
        out = total[:, :128]
        for c in range(128, ch, 128):
            out = out + total[:, c : c + 128]
        return out

    count = lax.fori_loop(0, chunks, setup, jnp.zeros((8, 128), jnp.float32))
    for it in range(ITERS):
        s_bl[it, me, 1] = count
    gains[0] = gains_in[...]

    pl.semaphore_wait(barrier, nb + nf - 2)

    def predict(it, target, arrivals):
        half = 2 * kb * chans
        misfit = jnp.zeros((8, 128), jnp.float32)
        for o in range(nb):
            if o > 0 and arrivals is not None:
                arrivals(o).wait_recv()
            first = bl_peer(o) * kb
            block = gains[it, :, pl.ds(first, kb)].reshape(half, stations)
            high, low = split_two(block)
            gsplit[o, 0] = high
            gsplit[o, 1] = low

            def step(i, misfit, o=o, first=first):
                at = pl.multiple_of(i * ch, ch)
                cols = pl.ds(at, ch)
                left = gsplit[o].reshape(2 * half, stations)
                right = pl.ds(pl.multiple_of(base + at, ch), ch)
                found = []
                for where in (cols, right):
                    both = jnp.dot(left, table[:, where], preferred_element_type=jnp.float32)
                    found.append((both[:half] + both[half:]).reshape(2, kb, chans, ch))
                    side[:, pl.ds(first, kb), :, where] = found[-1]
                source = vis if o == 0 else target
                er = [source[0, t, :, cols] for t in range(slots)]
                ei = [source[1, t, :, cols] for t in range(slots)]
                for kk in range(kb):
                    lr, li = found[0][0, kk], found[0][1, kk]
                    rr, ri = found[1][0, kk], found[1][1, kk]
                    pr = lr * rr + li * ri
                    pi = li * rr - lr * ri
                    for t in range(slots):
                        k = first + kk
                        sr, si = sky[0, k, t, :, cols], sky[1, k, t, :, cols]
                        er[t] = er[t] - (pr * sr - pi * si)
                        ei[t] = ei[t] - (pr * si + pi * sr)
                for t in range(slots):
                    target[0, t, :, cols] = er[t]
                    target[1, t, :, cols] = ei[t]
                    if o == nb - 1:
                        power = er[t] * er[t] + ei[t] * ei[t]
                        misfit = misfit + tile_sum(flag[t, :, cols].astype(jnp.float32) * power)
                return misfit

            misfit = lax.fori_loop(0, chunks, step, misfit)
        return misfit

    def gather_copy(it, o):
        block = gains.at[it, :, pl.ds(own, kb)]
        return remote(block, block, ag_send.at[it - 1, o], ag_recv.at[it - 1, o], "bl", bl_peer(o))

    def iteration(it, misfit, target=err, rhs_hook=None):
        s_bl[it, me, 0] = misfit
        copies = [
            remote(
                s_bl.at[it, me], s_bl.at[it, me], sb_send.at[it, o], sb_recv.at[it, o],
                "bl", bl_peer(o),
            )
            for o in range(1, nb)
        ]
        for copy in copies:
            copy.start()
        for copy in copies:
            copy.wait_recv()
        total = s_bl[it, 0]
        for o in range(1, nb):
            total = total + s_bl[it, o]
        s_fr[it, mf] = total
        more = [
            remote(
                s_fr.at[it, mf], s_fr.at[it, mf], sf_send.at[it, o], sf_recv.at[it, o],
                "freq", lax.rem(mf + o, nf),
            )
            for o in range(1, nf)
        ]
        for copy in more:
            copy.start()
        for copy in more:
            copy.wait_recv()
        total = s_fr[it, 0]
        for o in range(1, nf):
            total = total + s_fr[it, o]
        lanes = jnp.sum(total, axis=2, keepdims=True)
        sums = jnp.sum(lanes, axis=1, keepdims=True)
        sigma_sq = sums[0] / (sums[1] + 1.0) + small_term
        inverse = 1.0 / sigma_sq

        def weigh(i, carry):
            cols = pl.ds(pl.multiple_of(i * ch, ch), ch)
            total = None
            for t in range(slots):
                er, ei = err[0, t, :, cols], err[1, t, :, cols]
                power = er * er + ei * ei
                r = (
                    flag[t, :, cols].astype(jnp.float32)
                    * (robust_dof + 1.0)
                    / (robust_dof + power * inverse)
                )
                weighted[0, t, :, cols] = r * er
                weighted[1, t, :, cols] = r * ei
                total = r if total is None else total + r
            wsum[:, cols] = total
            return carry

        lax.fori_loop(0, chunks, weigh, 0)

        sends = []
        for o in reversed(range(nb)):
            owner = bl_peer(o)
            first = owner * kb

            def normal(i, carry, first=first):
                at = pl.multiple_of(i * ch, ch)
                cols = pl.ds(at, ch)
                right = pl.ds(pl.multiple_of(base + at, ch), ch)
                for kk in range(kb):
                    k = first + kk
                    lr, li = side[0, k, :, cols], side[1, k, :, cols]
                    rr, ri = side[0, k, :, right], side[1, k, :, right]
                    c2 = flux_sq[k] * wsum[:, cols]
                    xr = (lr * rr + li * ri) * c2
                    xi = (li * rr - lr * ri) * c2
                    for t in range(slots):
                        sr, si = sky[0, k, t, :, cols], sky[1, k, t, :, cols]
                        wr, wi = weighted[0, t, :, cols], weighted[1, t, :, cols]
                        xr = xr + (sr * wr + si * wi)
                        xi = xi + (sr * wi - si * wr)
                    terms = (
                        (rr * xr - ri * xi, lr * xr + li * xi),
                        (rr * xi + ri * xr, li * xr - lr * xi),
                        ((rr * rr + ri * ri) * c2, (lr * lr + li * li) * c2),
                    )
                    for q in range(3):
                        for s, where in enumerate((cols, right)):
                            high, low = split_two(terms[q][s])
                            stacked[0, q, kk, :, where] = high
                            stacked[1, q, kk, :, where] = low
                return carry

            lax.fori_loop(0, chunks, normal, 0)
            half = 3 * kb * chans
            both = lax.dot_general(
                stacked[...].reshape(2 * half, 2 * base),
                table[...],
                (((1,), (1,)), ((), ())),
                preferred_element_type=jnp.float32,
            )
            partial[it, o] = (both[:half] + both[half:]).reshape(3, kb, chans, stations)
            if o > 0:
                copy = remote(
                    partial.at[it, o], rs_buf.at[it, o], rs_send.at[it, o], rs_recv.at[it, o],
                    "bl", owner,
                )
                copy.start()
                sends.append(copy)
        for copy in sends:
            copy.wait_recv()

        for kk in range(kb):
            k = own + kk
            rho = penalty[k] * rho_scale
            sums_k = []
            for q in range(3):
                value = partial[it, 0, q, kk]
                for o in range(1, nb):
                    value = value + rs_buf[it, o, q, kk]
                sums_k.append(value)
            divisor = 1.0 / (sums_k[2] + rho)
            for c in range(2):
                anchor = -dual[c, k]
                for j in range(NPOLY):
                    anchor = anchor + basis[j] * cons_in[c, j, pl.ds(k, 1), :]
                solved = (sums_k[c] + rho * anchor) * divisor
                gains[it + 1, c, k] = 0.5 * (gains[it, c, k] + solved)
        spread = [gather_copy(it + 1, o) for o in range(1, nb)]
        for copy in spread:
            copy.start()
        if rhs_hook is not None:
            rhs_hook()
        result = predict(it + 1, target, lambda o: gather_copy(it + 1, o))
        for copy in copies + more + sends + spread:
            copy.wait_send()
        return result

    rows = 2 * NPOLY * kb
    grams = [(a, b) for a in range(NPOLY) for b in range(a + 1)]
    more = [
        remote(
            c_fr.at[mf], c_fr.at[mf], cf_send.at[o], cf_recv.at[o], "freq", lax.rem(mf + o, nf)
        )
        for o in range(1, nf)
    ]

    def project():
        for c in range(2):
            for kk in range(kb):
                both = gains[ITERS, c, own + kk] + dual[c, own + kk]
                for j in range(NPOLY):
                    row = (c * NPOLY + j) * kb + kk
                    c_fr[mf, row : row + 1, :] = jnp.sum(basis[j] * both, axis=0, keepdims=True)
        for n, (a, b) in enumerate(grams):
            entry = jnp.sum(basis[a] * basis[b], axis=0, keepdims=True)
            c_fr[mf, rows + n : rows + n + 1, :] = jnp.broadcast_to(entry, (1, stations))
        for row in range(rows + len(grams), c_fr.shape[1]):
            c_fr[mf, row : row + 1, :] = jnp.zeros((1, stations), jnp.float32)
        for copy in more:
            copy.start()

    misfit = lax.fori_loop(0, ITERS - 1, iteration, predict(0, err, None))
    iteration(ITERS - 1, misfit, resid_out, project)
    gains_out[...] = gains[ITERS]

    for copy in more:
        copy.wait_recv()
    total = c_fr[0]
    for o in range(1, nf):
        total = total + c_fr[o]
    gram = {ab: total[rows + n : rows + n + 1] for n, ab in enumerate(grams)}
    factor = {}
    for a in range(NPOLY):
        for b in range(a + 1):
            value = gram[a, b]
            for m in range(b):
                value = value - factor[a, m] * factor[b, m]
            factor[a, b] = jnp.sqrt(value) if a == b else value / factor[b, b]
    for c in range(2):
        part = [
            total[(c * NPOLY + j) * kb : (c * NPOLY + j + 1) * kb] for j in range(NPOLY)
        ]
        forward = []
        for a in range(NPOLY):
            running = part[a]
            for b in range(a):
                running = running - factor[a, b] * forward[b]
            forward.append(running / factor[a, a])
        backward = [None] * NPOLY
        for a in reversed(range(NPOLY)):
            running = forward[a]
            for b in range(a + 1, NPOLY):
                running = running - factor[b, a] * backward[b]
            backward[a] = running / factor[a, a]
        for j in range(NPOLY):
            row = (c * NPOLY + j) * kb
            c_bl[me, row : row + kb, :] = backward[j]
    for row in range(rows, c_bl.shape[1]):
        c_bl[me, row : row + 1, :] = jnp.zeros((1, stations), jnp.float32)
    spread = [
        remote(
            c_bl.at[me], c_bl.at[me], cb_send.at[o], cb_recv.at[o], "bl", bl_peer(o)
        )
        for o in range(1, nb)
    ]
    for copy in spread:
        copy.start()
    for copy in spread:
        copy.wait_recv()
    for g in range(nb):
        for kk in range(kb):
            k = g * kb + kk
            for c in range(2):
                value = dual[c, k] + gains[ITERS, c, k]
                for j in range(NPOLY):
                    row = (c * NPOLY + j) * kb + kk
                    coefficient = c_bl[g, row : row + 1, :]
                    cons_out[c, j, k : k + 1, :] = coefficient
                    value = value - basis[j] * coefficient
                dual_out[c, k] = value
    for copy in more + spread:
        copy.wait_send()


def body(nb, nf, vis, flag, pair, coords, dirs, flux, ratio, gains, dual, cons, penalty):
    f32, bf16 = jnp.float32, jnp.bfloat16
    _, slots, chans, base = vis.shape
    dirn, stations = gains.shape[1], gains.shape[3]
    kb = dirn // nb
    ch = 256
    rho_scale = 2.0 * base * nb * slots / stations
    sizes = (nb, nf, slots, chans, base, dirn, stations, ch, rho_scale)
    pad = lambda n: -(-n // 8) * 8
    rows = 2 * NPOLY * kb
    vmem = pl.BlockSpec(memory_space=pltpu.VMEM)
    smem = pl.BlockSpec(memory_space=pltpu.SMEM)
    dma = pltpu.SemaphoreType.DMA
    shape = jax.ShapeDtypeStruct
    return pl.pallas_call(
        functools.partial(kernel, sizes),
        name="admm_step",
        out_shape=(
            shape(gains.shape, f32),
            shape(cons.shape, f32),
            shape(dual.shape, f32),
            shape(vis.shape, f32),
        ),
        in_specs=[vmem, vmem, vmem, vmem, smem, vmem, vmem, vmem, vmem, vmem, smem],
        out_specs=(vmem, vmem, vmem, vmem),
        scratch_shapes=[
            pltpu.VMEM((stations, 2 * base), bf16),
            pltpu.VMEM((2, dirn, slots, chans, base), f32),
            pltpu.VMEM((2, dirn, chans, 2 * base), f32),
            pltpu.VMEM((nb, 2, 2 * kb * chans, stations), bf16),
            pltpu.VMEM((2, slots, chans, base), f32),
            pltpu.VMEM((2, slots, chans, base), f32),
            pltpu.VMEM((chans, base), f32),
            pltpu.VMEM((dirn, chans, ch), f32),
            pltpu.VMEM((2, 3, kb, chans, 2 * base), bf16),
            pltpu.VMEM((ITERS, nb, 3, kb, chans, stations), f32),
            pltpu.VMEM((ITERS, nb, 3, kb, chans, stations), f32),
            pltpu.VMEM((ITERS + 1,) + gains.shape, f32),
            pltpu.VMEM((ITERS, nb, 2, 8, 128), f32),
            pltpu.VMEM((ITERS, nf, 2, 8, 128), f32),
            pltpu.VMEM((nf, pad(rows + 6), stations), f32),
            pltpu.VMEM((nb, pad(rows), stations), f32),
            dma((ITERS, nb)),
            dma((ITERS, nb)),
            dma((ITERS, nb)),
            dma((ITERS, nb)),
            dma((ITERS, nb)),
            dma((ITERS, nb)),
            dma((ITERS, nf)),
            dma((ITERS, nf)),
            dma((nf,)),
            dma((nf,)),
            dma((nb,)),
            dma((nb,)),
        ],
        compiler_params=pltpu.CompilerParams(
            collective_id=0, has_side_effects=True, vmem_limit_bytes=60 * 1024 * 1024
        ),
    )(vis, flag, pair, coords, dirs, flux, ratio.reshape(1, -1), gains, dual, cons, penalty)


def solution(mesh):
    in_specs = (
        P(None, None, "freq", "bl"),
        P(None, "freq", "bl"),
        P(None, "bl"),
        P(None, None, "bl"),
        P(),
        P(None, "freq"),
        P("freq"),
        P(None, None, "freq", None),
        P(None, None, "freq", None),
        P(),
        P(),
    )
    out_specs = (
        P(None, None, "freq", None),
        P(),
        P(None, None, "freq", None),
        P(None, None, "freq", "bl"),
    )
    step = functools.partial(body, mesh.shape["bl"], mesh.shape["freq"])
    return jax.shard_map(step, mesh=mesh, in_specs=in_specs, out_specs=out_specs, check_vma=False)
```

```python
import functools
import math

import jax
import jax.numpy as jnp
from jax import lax
from jax.experimental import pallas as pl
from jax.experimental.pallas import tpu as pltpu
from jax.sharding import PartitionSpec as P

NPOLY = 3
ITERS = 3

robust_dof = 2.0
small_term = 1e-06
two_pi = 2.0 * math.pi
MESH = pl.DeviceIdType.MESH

SIN_TERMS = [(-1.0) ** n * two_pi ** (2 * n + 1) / math.factorial(2 * n + 1) for n in range(6)]
COS_TERMS = [(-1.0) ** n * two_pi ** (2 * n) / math.factorial(2 * n) for n in range(7)]


def horner(terms, square):
    value = jnp.full_like(square, terms[-1])
    for term in terms[-2::-1]:
        value = value * square + term
    return value


def turn_parts(turns):
    half = jnp.floor(turns * 2.0 + 0.5)
    rest = turns - half * 0.5
    sign = 1.0 - 2.0 * (half - 2.0 * jnp.floor(half * 0.5))
    square = rest * rest
    return horner(COS_TERMS, square), rest * horner(SIN_TERMS, square), sign


def column(row, count):
    spread = jnp.broadcast_to(row, (count, count))
    r = lax.broadcasted_iota(jnp.int32, (count, count), 0)
    c = lax.broadcasted_iota(jnp.int32, (count, count), 1)
    return jnp.sum(jnp.where(r == c, spread, 0.0), axis=1, keepdims=True)


def split_two(value):
    high = value.astype(jnp.bfloat16)
    low = (value - high.astype(jnp.float32)).astype(jnp.bfloat16)
    return high, low


def kernel(
    sizes,
    vis,
    flag,
    pair,
    coords,
    dirs,
    flux,
    ratio,
    gains_in,
    dual,
    cons_in,
    penalty,
    gains_out,
    cons_out,
    dual_out,
    resid_out,
    table,
    sky,
    side,
    gsplit,
    err,
    weighted,
    wsum,
    flux_sq,
    stacked,
    partial,
    rs_buf,
    gains,
    s_bl,
    s_fr,
    c_fr,
    c_bl,
    rs_send,
    rs_recv,
    ag_send,
    ag_recv,
    sb_send,
    sb_recv,
    sf_send,
    sf_recv,
    cf_send,
    cf_recv,
    cb_send,
    cb_recv,
):
    nb, nf, slots, chans, base, dirn, stations, ch, rho_scale = sizes
    kb = dirn // nb
    chunks = base // ch
    me = lax.axis_index("bl")
    mf = lax.axis_index("freq")
    own = me * kb

    def bl_peer(o):
        return lax.bitwise_xor(me, o)

    barrier = pltpu.get_barrier_semaphore()
    for o in range(1, nb):
        pl.semaphore_signal(
            barrier, inc=1, device_id={"bl": bl_peer(o)}, device_id_type=MESH
        )
    for o in range(1, nf):
        pl.semaphore_signal(
            barrier, inc=1, device_id={"freq": lax.rem(mf + o, nf)}, device_id_type=MESH
        )

    def remote(src, dst, send, recv, axis, target):
        return pltpu.make_async_remote_copy(
            src_ref=src,
            dst_ref=dst,
            send_sem=send,
            recv_sem=recv,
            device_id={axis: target},
            device_id_type=MESH,
        )

    ratio_col = column(ratio[...], chans)
    scaled = (ratio_col - 1.05) / 0.35
    basis = [jnp.ones_like(scaled), scaled, (3.0 * scaled * scaled - 1.0) / 2.0]
    flux_cols = [column(flux[k : k + 1, :], chans) for k in range(dirn)]
    for k in range(dirn):
        flux_sq[k] = jnp.broadcast_to(flux_cols[k] * flux_cols[k], (chans, ch))

    def setup(i, count):
        at = pl.multiple_of(i * ch, ch)
        cols = pl.ds(at, ch)
        rows = lax.broadcasted_iota(jnp.int32, (stations, ch), 0)
        for s in range(2):
            hit = rows == pair[s : s + 1, cols]
            table[:, pl.ds(pl.multiple_of(s * base + at, ch), ch)] = jnp.where(
                hit, 1.0, 0.0
            ).astype(jnp.bfloat16)
        for t in range(slots):
            u = coords[0, t : t + 1, cols]
            v = coords[1, t : t + 1, cols]
            for k in range(dirn):
                project = dirs[0, k] * u + dirs[1, k] * v
                cosine, sine, sign = turn_parts(project * ratio_col)
                amplitude = sign * flux_cols[k]
                sky[0, k, t, :, cols] = amplitude * cosine
                sky[1, k, t, :, cols] = amplitude * sine
            count = count + tile_sum(flag[t, :, cols].astype(jnp.float32))
        return count

    def tile_sum(value):
        total = value[:8]
        for r in range(8, chans, 8):
            total = total + value[r : r + 8]
        out = total[:, :128]
        for c in range(128, ch, 128):
            out = out + total[:, c : c + 128]
        return out

    count = lax.fori_loop(0, chunks, setup, jnp.zeros((8, 128), jnp.float32))
    for it in range(ITERS):
        s_bl[it, me, 1:2] = jnp.sum(count, axis=0, keepdims=True)
    gains[0] = gains_in[...]

    pl.semaphore_wait(barrier, nb + nf - 2)

    def predict(it, target, arrivals):
        half = 2 * kb * chans
        misfit = jnp.zeros((8, 128), jnp.float32)
        for o in range(nb):
            if o > 0 and arrivals is not None:
                arrivals(o).wait_recv()
            first = bl_peer(o) * kb
            block = gains[it, :, pl.ds(first, kb)].reshape(half, stations)
            high, low = split_two(block)
            gsplit[o, 0] = high
            gsplit[o, 1] = low

            def step(i, misfit, o=o, first=first):
                at = pl.multiple_of(i * ch, ch)
                cols = pl.ds(at, ch)
                left = gsplit[o].reshape(2 * half, stations)
                right = pl.ds(pl.multiple_of(base + at, ch), ch)
                found = []
                for where in (cols, right):
                    both = jnp.dot(left, table[:, where], preferred_element_type=jnp.float32)
                    found.append((both[:half] + both[half:]).reshape(2, kb, chans, ch))
                    side[:, pl.ds(first, kb), :, where] = found[-1]
                source = vis if o == 0 else target
                er = [source[0, t, :, cols] for t in range(slots)]
                ei = [source[1, t, :, cols] for t in range(slots)]
                for kk in range(kb):
                    lr, li = found[0][0, kk], found[0][1, kk]
                    rr, ri = found[1][0, kk], found[1][1, kk]
                    pr = lr * rr + li * ri
                    pi = li * rr - lr * ri
                    for t in range(slots):
                        k = first + kk
                        sr, si = sky[0, k, t, :, cols], sky[1, k, t, :, cols]
                        er[t] = er[t] - (pr * sr - pi * si)
                        ei[t] = ei[t] - (pr * si + pi * sr)
                for t in range(slots):
                    target[0, t, :, cols] = er[t]
                    target[1, t, :, cols] = ei[t]
                    if o == nb - 1:
                        power = er[t] * er[t] + ei[t] * ei[t]
                        misfit = misfit + tile_sum(flag[t, :, cols].astype(jnp.float32) * power)
                return misfit

            misfit = lax.fori_loop(0, chunks, step, misfit)
        return misfit

    def gather_copy(it, o):
        block = gains.at[it, :, pl.ds(own, kb)]
        return remote(block, block, ag_send.at[it - 1, o], ag_recv.at[it - 1, o], "bl", bl_peer(o))

    def iteration(it, misfit, target=err, rhs_hook=None):
        s_bl[it, me, 0:1] = jnp.sum(misfit, axis=0, keepdims=True)
        copies = [
            remote(
                s_bl.at[it, me], s_bl.at[it, me], sb_send.at[it, o], sb_recv.at[it, o],
                "bl", bl_peer(o),
            )
            for o in range(1, nb)
        ]
        for copy in copies:
            copy.start()
        for copy in copies:
            copy.wait_recv()
        total = s_bl[it, 0]
        for o in range(1, nb):
            total = total + s_bl[it, o]
        s_fr[it, mf] = total
        more = [
            remote(
                s_fr.at[it, mf], s_fr.at[it, mf], sf_send.at[it, o], sf_recv.at[it, o],
                "freq", lax.rem(mf + o, nf),
            )
            for o in range(1, nf)
        ]
        for copy in more:
            copy.start()
        for copy in more:
            copy.wait_recv()
        total = s_fr[it, 0]
        for o in range(1, nf):
            total = total + s_fr[it, o]
        sums = jnp.sum(total, axis=1, keepdims=True)
        sigma_sq = sums[0:1] / (sums[1:2] + 1.0) + small_term
        inverse = 1.0 / sigma_sq

        def weigh(i, carry):
            cols = pl.ds(pl.multiple_of(i * ch, ch), ch)
            total = None
            for t in range(slots):
                er, ei = err[0, t, :, cols], err[1, t, :, cols]
                power = er * er + ei * ei
                r = (
                    flag[t, :, cols].astype(jnp.float32)
                    * (robust_dof + 1.0)
                    / (robust_dof + power * inverse)
                )
                weighted[0, t, :, cols] = r * er
                weighted[1, t, :, cols] = r * ei
                total = r if total is None else total + r
            wsum[:, cols] = total
            return carry

        lax.fori_loop(0, chunks, weigh, 0)

        sends = []
        for o in reversed(range(nb)):
            owner = bl_peer(o)
            first = owner * kb

            def normal(i, carry, first=first):
                at = pl.multiple_of(i * ch, ch)
                cols = pl.ds(at, ch)
                right = pl.ds(pl.multiple_of(base + at, ch), ch)
                for kk in range(kb):
                    k = first + kk
                    lr, li = side[0, k, :, cols], side[1, k, :, cols]
                    rr, ri = side[0, k, :, right], side[1, k, :, right]
                    c2 = flux_sq[k] * wsum[:, cols]
                    xr = (lr * rr + li * ri) * c2
                    xi = (li * rr - lr * ri) * c2
                    for t in range(slots):
                        sr, si = sky[0, k, t, :, cols], sky[1, k, t, :, cols]
                        wr, wi = weighted[0, t, :, cols], weighted[1, t, :, cols]
                        xr = xr + (sr * wr + si * wi)
                        xi = xi + (sr * wi - si * wr)
                    terms = (
                        (rr * xr - ri * xi, lr * xr + li * xi),
                        (rr * xi + ri * xr, li * xr - lr * xi),
                        ((rr * rr + ri * ri) * c2, (lr * lr + li * li) * c2),
                    )
                    for q in range(3):
                        for s, where in enumerate((cols, right)):
                            high, low = split_two(terms[q][s])
                            stacked[0, q, kk, :, where] = high
                            stacked[1, q, kk, :, where] = low
                return carry

            lax.fori_loop(0, chunks, normal, 0)
            half = 3 * kb * chans
            both = lax.dot_general(
                stacked[...].reshape(2 * half, 2 * base),
                table[...],
                (((1,), (1,)), ((), ())),
                preferred_element_type=jnp.float32,
            )
            partial[it, o] = (both[:half] + both[half:]).reshape(3, kb, chans, stations)
            if o > 0:
                copy = remote(
                    partial.at[it, o], rs_buf.at[it, o], rs_send.at[it, o], rs_recv.at[it, o],
                    "bl", owner,
                )
                copy.start()
                sends.append(copy)
        for copy in sends:
            copy.wait_recv()

        for kk in range(kb):
            k = own + kk
            rho = penalty[k] * rho_scale
            sums_k = []
            for q in range(3):
                value = partial[it, 0, q, kk]
                for o in range(1, nb):
                    value = value + rs_buf[it, o, q, kk]
                sums_k.append(value)
            divisor = 1.0 / (sums_k[2] + rho)
            for c in range(2):
                anchor = -dual[c, k]
                for j in range(NPOLY):
                    anchor = anchor + basis[j] * cons_in[c, j, pl.ds(k, 1), :]
                solved = (sums_k[c] + rho * anchor) * divisor
                gains[it + 1, c, k] = 0.5 * (gains[it, c, k] + solved)
        spread = [gather_copy(it + 1, o) for o in range(1, nb)]
        for copy in spread:
            copy.start()
        if rhs_hook is not None:
            rhs_hook()
        result = predict(it + 1, target, lambda o: gather_copy(it + 1, o))
        for copy in copies + more + sends + spread:
            copy.wait_send()
        return result

    rows = 2 * NPOLY * kb
    grams = [(a, b) for a in range(NPOLY) for b in range(a + 1)]
    more = [
        remote(
            c_fr.at[mf], c_fr.at[mf], cf_send.at[o], cf_recv.at[o], "freq", lax.rem(mf + o, nf)
        )
        for o in range(1, nf)
    ]

    def project():
        for c in range(2):
            for kk in range(kb):
                both = gains[ITERS, c, own + kk] + dual[c, own + kk]
                for j in range(NPOLY):
                    row = (c * NPOLY + j) * kb + kk
                    c_fr[mf, row : row + 1, :] = jnp.sum(basis[j] * both, axis=0, keepdims=True)
        for n, (a, b) in enumerate(grams):
            entry = jnp.sum(basis[a] * basis[b], axis=0, keepdims=True)
            c_fr[mf, rows + n : rows + n + 1, :] = jnp.broadcast_to(entry, (1, stations))
        for row in range(rows + len(grams), c_fr.shape[1]):
            c_fr[mf, row : row + 1, :] = jnp.zeros((1, stations), jnp.float32)
        for copy in more:
            copy.start()

    misfit = lax.fori_loop(0, ITERS - 1, iteration, predict(0, err, None))
    iteration(ITERS - 1, misfit, resid_out, project)
    gains_out[...] = gains[ITERS]

    for copy in more:
        copy.wait_recv()
    total = c_fr[0]
    for o in range(1, nf):
        total = total + c_fr[o]
    gram = {ab: total[rows + n : rows + n + 1] for n, ab in enumerate(grams)}
    factor = {}
    for a in range(NPOLY):
        for b in range(a + 1):
            value = gram[a, b]
            for m in range(b):
                value = value - factor[a, m] * factor[b, m]
            factor[a, b] = jnp.sqrt(value) if a == b else value / factor[b, b]
    for c in range(2):
        part = [
            total[(c * NPOLY + j) * kb : (c * NPOLY + j + 1) * kb] for j in range(NPOLY)
        ]
        forward = []
        for a in range(NPOLY):
            running = part[a]
            for b in range(a):
                running = running - factor[a, b] * forward[b]
            forward.append(running / factor[a, a])
        backward = [None] * NPOLY
        for a in reversed(range(NPOLY)):
            running = forward[a]
            for b in range(a + 1, NPOLY):
                running = running - factor[b, a] * backward[b]
            backward[a] = running / factor[a, a]
        for j in range(NPOLY):
            row = (c * NPOLY + j) * kb
            c_bl[me, row : row + kb, :] = backward[j]
    for row in range(rows, c_bl.shape[1]):
        c_bl[me, row : row + 1, :] = jnp.zeros((1, stations), jnp.float32)
    spread = [
        remote(
            c_bl.at[me], c_bl.at[me], cb_send.at[o], cb_recv.at[o], "bl", bl_peer(o)
        )
        for o in range(1, nb)
    ]
    for copy in spread:
        copy.start()
    for copy in spread:
        copy.wait_recv()
    for g in range(nb):
        for kk in range(kb):
            k = g * kb + kk
            for c in range(2):
                value = dual[c, k] + gains[ITERS, c, k]
                for j in range(NPOLY):
                    row = (c * NPOLY + j) * kb + kk
                    coefficient = c_bl[g, row : row + 1, :]
                    cons_out[c, j, k : k + 1, :] = coefficient
                    value = value - basis[j] * coefficient
                dual_out[c, k] = value
    for copy in more + spread:
        copy.wait_send()


def body(nb, nf, vis, flag, pair, coords, dirs, flux, ratio, gains, dual, cons, penalty):
    f32, bf16 = jnp.float32, jnp.bfloat16
    _, slots, chans, base = vis.shape
    dirn, stations = gains.shape[1], gains.shape[3]
    kb = dirn // nb
    ch = 256
    rho_scale = 2.0 * base * nb * slots / stations
    sizes = (nb, nf, slots, chans, base, dirn, stations, ch, rho_scale)
    pad = lambda n: -(-n // 8) * 8
    rows = 2 * NPOLY * kb
    vmem = pl.BlockSpec(memory_space=pltpu.VMEM)
    smem = pl.BlockSpec(memory_space=pltpu.SMEM)
    dma = pltpu.SemaphoreType.DMA
    shape = jax.ShapeDtypeStruct
    return pl.pallas_call(
        functools.partial(kernel, sizes),
        name="admm_step",
        out_shape=(
            shape(gains.shape, f32),
            shape(cons.shape, f32),
            shape(dual.shape, f32),
            shape(vis.shape, f32),
        ),
        in_specs=[vmem, vmem, vmem, vmem, smem, vmem, vmem, vmem, vmem, vmem, smem],
        out_specs=(vmem, vmem, vmem, vmem),
        scratch_shapes=[
            pltpu.VMEM((stations, 2 * base), bf16),
            pltpu.VMEM((2, dirn, slots, chans, base), f32),
            pltpu.VMEM((2, dirn, chans, 2 * base), f32),
            pltpu.VMEM((nb, 2, 2 * kb * chans, stations), bf16),
            pltpu.VMEM((2, slots, chans, base), f32),
            pltpu.VMEM((2, slots, chans, base), f32),
            pltpu.VMEM((chans, base), f32),
            pltpu.VMEM((dirn, chans, ch), f32),
            pltpu.VMEM((2, 3, kb, chans, 2 * base), bf16),
            pltpu.VMEM((ITERS, nb, 3, kb, chans, stations), f32),
            pltpu.VMEM((ITERS, nb, 3, kb, chans, stations), f32),
            pltpu.VMEM((ITERS + 1,) + gains.shape, f32),
            pltpu.VMEM((ITERS, nb, 2, 128), f32),
            pltpu.VMEM((ITERS, nf, 2, 128), f32),
            pltpu.VMEM((nf, pad(rows + 6), stations), f32),
            pltpu.VMEM((nb, pad(rows), stations), f32),
            dma((ITERS, nb)),
            dma((ITERS, nb)),
            dma((ITERS, nb)),
            dma((ITERS, nb)),
            dma((ITERS, nb)),
            dma((ITERS, nb)),
            dma((ITERS, nf)),
            dma((ITERS, nf)),
            dma((nf,)),
            dma((nf,)),
            dma((nb,)),
            dma((nb,)),
        ],
        compiler_params=pltpu.CompilerParams(
            collective_id=0, has_side_effects=True, vmem_limit_bytes=60 * 1024 * 1024
        ),
    )(vis, flag, pair, coords, dirs, flux, ratio.reshape(1, -1), gains, dual, cons, penalty)


def solution(mesh):
    in_specs = (
        P(None, None, "freq", "bl"),
        P(None, "freq", "bl"),
        P(None, "bl"),
        P(None, None, "bl"),
        P(),
        P(None, "freq"),
        P("freq"),
        P(None, None, "freq", None),
        P(None, None, "freq", None),
        P(),
        P(),
    )
    out_specs = (
        P(None, None, "freq", None),
        P(),
        P(None, None, "freq", None),
        P(None, None, "freq", "bl"),
    )
    step = functools.partial(body, mesh.shape["bl"], mesh.shape["freq"])
    return jax.shard_map(step, mesh=mesh, in_specs=in_specs, out_specs=out_specs, check_vma=False)
```
